32 devices in a mesh: groups: 2 (over x), depth: 8 (over z, y), height: 2 (over core).
Axes of the slice: x: 2, y: 2, z: 4, core: 2. Of those that a mesh axis runs over, the one named last changes fastest.
Arguments:
- images: bfloat16 [4, 4, 64, 16, 256], P('groups', None, 'depth', 'height'), parts along dimension 0, may hold values from -6 to 6
- pre_hidden: bfloat16 [4, 16, 64, 16, 256], P('groups', None, 'depth', 'height'), parts along dimension 0, may hold values from -6 to 6
- pre_deep: bfloat16 [4, 32, 32, 8, 128], P(('groups', 'height'), None, 'depth'), parts along dimension 0, may hold values from -6 to 6
- pooled_grad: bfloat16 [4, 32, 16, 256], P(('groups', 'height'), None, 'depth'), parts along dimension 0, may hold values from -1.25 to 1.25
- deep_weight: bfloat16 [32, 16, 3, 3, 3], replicated, may hold values from -0.3125 to 0.3125
Outputs:
- first_kernel: float32 [32, 4, 3, 3, 3], P('groups'), parts along dimension 0
- first_bias: float32 [32], P('groups'), parts along dimension 0
- deep_kernel: float32 [64, 16, 3, 3, 3], P('groups'), parts along dimension 0
- deep_bias: float32 [64], P('groups'), parts along dimension 0
The draws below stay inside these ranges and needn't reach their ends.
There are 2 independent parts, one for each index of `groups`. The reference program is written for one: setup_inputs(seed, part) draws one part's arguments, and reference() takes and returns one part's arrays. A program takes and returns all parts, laid end to end along the dimension named above; an argument that names none is the same for every part. Nothing has to cross between parts.
All inputs are finite; a program needn't handle non-finite values.
Results may differ from the reference program's by a relative error of at most 0.0031.
Values may be sent and summed in bfloat16 or wider, within the bound.
A program may use at most 128 MiB of HBM per device.

```python
import jax
import jax.numpy as jnp
from jax import lax

CHAN_IN = 4
CHAN_MID = 16
CHAN_OUT = 32
SAMPLES = 2
HEIGHT = 16
WIDTH = 256
DEPTH = 64


def block_levels(own_key, extent, shards, smallest, largest):
    def one(position, parts):
        heights = jax.random.uniform(jax.random.fold_in(jax.random.fold_in(own_key, 6), position), (parts,), jnp.float32, smallest / len(shards), largest / len(shards))
        return jnp.repeat(jnp.exp(heights), extent[position] // parts).reshape((-1,) + (1,) * (len(extent) - position - 1))

    gain = one(*shards[0])
    for cut in shards[1:]:
        gain = gain * one(*cut)
    return gain


def scatter_about(key, dims, scale, limit, cuts=(), kind=jnp.bfloat16):
    entries = jax.random.normal(key, dims, jnp.float32) * scale
    if len(cuts) > 0:
        entries = block_levels(key, dims, cuts, -0.22, 0.18) * entries
    return jnp.clip(entries, min=-limit, max=limit).astype(kind)


def setup_inputs(seed: int = 0, part: int = 0) -> dict:
    key_list = jax.random.split(jax.random.key(seed), 6)
    part_splits = jax.random.split(jax.random.fold_in(key_list[5], part), 6)
    images = scatter_about(part_splits[0], (SAMPLES, CHAN_IN, DEPTH, HEIGHT, WIDTH), 1.0, 6.0, ((2, 8), (3, 2)))
    pre_hidden = scatter_about(part_splits[1], (SAMPLES, CHAN_MID, DEPTH, HEIGHT, WIDTH), 1.0, 6.0, ((2, 8), (3, 2)))
    pre_deep = scatter_about(part_splits[2], (SAMPLES, CHAN_OUT, DEPTH // 2, HEIGHT // 2, WIDTH // 2), 1.0, 6.0, ((0, 2), (2, 8)))
    pooled_grad = scatter_about(part_splits[3], (SAMPLES, CHAN_OUT, DEPTH // 4, (HEIGHT // 4) * (WIDTH // 4)), (20 * (SAMPLES * DEPTH * HEIGHT * WIDTH // 8) ** -0.5), 1.25, ((0, 2), (2, 8)))
    deep_weight = scatter_about(key_list[4], (CHAN_OUT, CHAN_MID, 3, 3, 3), (CHAN_MID * 27) ** -0.5, 0.3125)
    return {"images": images, "pre_hidden": pre_hidden, "pre_deep": pre_deep, "pooled_grad": pooled_grad, "deep_weight": deep_weight}


SLOPE = 0.3


def leaky(values):
    return jnp.where(values > 0, values, SLOPE * values)


def slope_at(values):
    return jnp.where(values > 0, 1.0, SLOPE)


def reference(images, pre_hidden, pre_deep, pooled_grad, deep_weight):
    samples = images.shape[0]
    coarse = pooled_grad.astype(jnp.float32).reshape(samples, CHAN_OUT, DEPTH // 4, HEIGHT // 4, WIDTH // 4) / 8.0
    spread = jnp.repeat(jnp.repeat(jnp.repeat(coarse, 2, axis=2), 2, axis=3), 2, axis=4)
    deep_grad = (spread * slope_at(pre_deep.astype(jnp.float32))).astype(jnp.bfloat16)
    hidden = leaky(pre_hidden.astype(jnp.float32)).astype(jnp.bfloat16)
    padded = jnp.pad(hidden, ((0, 0), (0, 0), (1, 0), (1, 0), (1, 0)))
    deep_float = deep_grad.astype(jnp.float32)
    kernels = []
    total = None
    for depth_tap in range(3):
        for height_tap in range(3):
            for width_tap in range(3):
                view = padded[:, :, depth_tap:depth_tap + DEPTH - 1:2, height_tap:height_tap + HEIGHT - 1:2, width_tap:width_tap + WIDTH - 1:2]
                kernels.append(jnp.einsum("sodhw,sidhw->oi", deep_float, view.astype(jnp.float32)))
                term = jnp.einsum("oi,sodhw->sidhw", deep_weight[:, :, depth_tap, height_tap, width_tap].astype(jnp.float32), deep_float)
                placed = lax.pad(term, jnp.zeros((), term.dtype), ((0, 0, 0), (0, 0, 0), (depth_tap, 2 - depth_tap, 1), (height_tap, 2 - height_tap, 1), (width_tap, 2 - width_tap, 1)))
                total = placed if total is None else total + placed
    deep_kernel = jnp.stack(kernels, axis=-1).reshape(CHAN_OUT, CHAN_MID, 3, 3, 3)
    deep_bias = jnp.sum(deep_float, axis=(0, 2, 3, 4))
    hidden_grad = total[:, :, 1:, 1:, 1:].astype(jnp.bfloat16)
    first_grad = (hidden_grad.astype(jnp.float32) * slope_at(pre_hidden.astype(jnp.float32))).astype(jnp.bfloat16)
    framed = jnp.pad(images, ((0, 0), (0, 0), (1, 1), (1, 1), (1, 1)))
    first_float = first_grad.astype(jnp.float32)
    firsts = []
    for depth_tap in range(3):
        for height_tap in range(3):
            for width_tap in range(3):
                view = framed[:, :, depth_tap:depth_tap + DEPTH, height_tap:height_tap + HEIGHT, width_tap:width_tap + WIDTH]
                firsts.append(jnp.einsum("sodhw,sidhw->oi", first_float, view.astype(jnp.float32)))
    first_kernel = jnp.stack(firsts, axis=-1).reshape(CHAN_MID, CHAN_IN, 3, 3, 3)
    first_bias = jnp.sum(first_float, axis=(0, 2, 3, 4))
    return (first_kernel, first_bias, deep_kernel, deep_bias)
```

```python
import functools

import jax
import jax.numpy as jnp
from jax import lax
from jax.experimental import pallas as pl
from jax.experimental.pallas import tpu as pltpu
from jax.sharding import PartitionSpec as P

SLOPE = 0.3
MESH = pl.DeviceIdType.MESH
BF = jnp.bfloat16
F32 = jnp.float32
TAP = ((1, 1), (0, 0), (0, 1))


def vmem():
    return pl.BlockSpec(memory_space=pltpu.VMEM)


def iota(shape, dim):
    return lax.broadcasted_iota(jnp.int32, shape, dim)


def one_hot(row_target, shape):
    return jnp.where(row_target == iota(shape, 1), 1.0, 0.0).astype(BF)


def dot(a, b):
    return jnp.dot(a, b, preferred_element_type=F32)


def dot_nt(a, b):
    return lax.dot_general(a, b, (((1,), (1,)), ((), ())), preferred_element_type=F32)


def exchange_kernel(count, img, pd, pool, img_all, pd_all, pool_all, send, recv):
    k = lax.axis_index("depth")
    h = lax.axis_index("height")
    cells = img.shape[2]
    quarter = pd.shape[1]
    barrier = pltpu.get_barrier_semaphore()

    def greet(depth, height):
        pl.semaphore_signal(
            barrier, inc=1, device_id={"depth": depth, "height": height}, device_id_type=MESH
        )

    greet(k, 1 - h)

    @pl.when(k > 0)
    def _():
        greet(k - 1, 0)
        greet(k - 1, 1)

    @pl.when(k < count - 1)
    def _():
        greet(k + 1, 0)
        greet(k + 1, 1)

    pl.semaphore_wait(barrier, 1 + 2 * ((k + count - 1) // count + (2 * count - 2 - k) // count))

    def copy(src, dst, send_slot, recv_slot, depth, height):
        return pltpu.make_async_remote_copy(
            src_ref=src,
            dst_ref=dst,
            send_sem=send.at[send_slot],
            recv_sem=recv.at[recv_slot],
            device_id={"depth": depth, "height": height},
            device_id_type=MESH,
        )

    def partner(slot):
        return [
            copy(pd, pd_all.at[slot, :, 0:quarter], 0, 0, k, 1 - h),
            copy(pool, pool_all.at[slot, 0], 1, 1, k, 1 - h),
            copy(img, img_all.at[slot, :, :, 1 : cells + 1], 2, 2, k, 1 - h),
        ]

    def down(slot, height):
        base = 3 + 3 * height
        arrive = 3 + 3 * slot
        return [
            copy(pd.at[:, 0:1], pd_all.at[slot, :, quarter : quarter + 1], base, arrive, k - 1, height),
            copy(pool, pool_all.at[slot, 1], base + 1, arrive + 1, k - 1, height),
            copy(img.at[:, :, 0:1], img_all.at[slot, :, :, cells + 1 : cells + 2], base + 2, arrive + 2, k - 1, height),
        ]

    def up(slot, height):
        return [
            copy(img.at[:, :, cells - 1 : cells], img_all.at[slot, :, :, 0:1], 9 + height, 9 + slot, k + 1, height)
        ]

    @pl.when(k > 0)
    def _():
        for height in range(2):
            for c in down(h, height):
                c.start()

    @pl.when(k < count - 1)
    def _():
        for height in range(2):
            for c in up(h, height):
                c.start()

    for c in partner(h):
        c.start()
    img_all[h, :, :, 1 : cells + 1] = img[...]
    pd_all[h, :, 0:quarter] = pd[...]
    pool_all[h, 0] = pool[...]

    @pl.when(k == 0)
    def _():
        img_all[:, :, :, 0:1] = jnp.zeros_like(img_all[:, :, :, 0:1])

    @pl.when(k == count - 1)
    def _():
        img_all[:, :, :, cells + 1 : cells + 2] = jnp.zeros_like(img_all[:, :, :, 0:1])
        pd_all[:, :, quarter : quarter + 1] = jnp.zeros_like(pd_all[:, :, 0:1])
        pool_all[:, 1] = jnp.zeros_like(pool_all[:, 1])

    for c in partner(h):
        c.wait_send()
    for c in partner(1 - h):
        c.wait_recv()

    @pl.when(k > 0)
    def _():
        for height in range(2):
            for c in down(h, height):
                c.wait_send()
            for c in up(height, height):
                c.wait_recv()

    @pl.when(k < count - 1)
    def _():
        for height in range(2):
            for c in up(h, height):
                c.wait_send()
            for c in down(height, height):
                c.wait_recv()


def exchange(count, images, pre_deep, pooled):
    samples, chans, cells, rows, width = images.shape
    out_chans, coarse, coarse_rows, coarse_width = pre_deep.shape
    return pl.pallas_call(
        functools.partial(exchange_kernel, count),
        out_shape=(
            jax.ShapeDtypeStruct((2, samples, chans, cells + 2, rows, width), BF),
            jax.ShapeDtypeStruct((2, out_chans, coarse + 1, coarse_rows, coarse_width), BF),
            jax.ShapeDtypeStruct((2, 2) + pooled.shape, BF),
        ),
        in_specs=[vmem()] * 3,
        out_specs=(vmem(),) * 3,
        scratch_shapes=[pltpu.SemaphoreType.DMA((11,)), pltpu.SemaphoreType.DMA((11,))],
        compiler_params=pltpu.CompilerParams(collective_id=0, has_side_effects=True),
    )(images, pre_deep, pooled)


def compute_kernel(hid, img, pd, pool, weight, out, ph_buf, g_buf, i_buf):
    me = lax.axis_index("height")

    def cell(s, d2, h2):
        at = ((s * 4 + d2) * 4 + h2) * 128
        return slice(at, at + 128)

    row = iota((128, 128), 0)
    order = one_hot((row & 15) * 8 + (row >> 4), (128, 128))
    z = iota((256, 256), 0)
    col = iota((256, 256), 1)
    split = jnp.where(z == 2 * (col & 127) + (col >> 7), 1.0, 0.0).astype(BF)
    for s in range(2):
        for d in range(8):
            x = hid[s, :, d].astype(F32).reshape(128, 256).astype(BF)
            a = dot(x, split).astype(BF)
            b = dot(order, a).astype(BF)
            for h2 in range(4):
                for pw in range(2):
                    r = (d % 2) * 64 + pw * 32
                    ph_buf[r : r + 32, cell(s, d // 2, h2)] = b[
                        h2 * 32 : h2 * 32 + 32, pw * 128 : pw * 128 + 128
                    ]

    row = iota((160, 256), 0)
    high = 4 * me + (row >> 5)
    pick = one_hot(jnp.where(high < 8, (row & 31) * 8 + high, -1), (160, 256))
    r640 = iota((256, 640), 0)
    c640 = iota((256, 640), 1)
    spread_mat = jnp.where(
        r640 == ((4 * me + (c640 >> 7)) >> 1) * 64 + ((c640 & 127) >> 1), 1.0, 0.0
    ).astype(BF)
    lane = iota((32, 128), 1)
    deep_sum = jnp.zeros((32, 128), F32)
    for s in range(2):
        for d in range(5):
            if d % 2 == 0:
                coarse = pool[s, d // 4].astype(F32)[:, (d // 2) % 2, :].astype(BF)
                spread = dot(coarse, spread_mat) / 8.0
            x = pd[s, :, d].astype(F32).reshape(256, 128).astype(BF)
            y = dot(pick, x)
            for j in range(5):
                slope = jnp.where(y[j * 32 : j * 32 + 32] > 0, 1.0, SLOPE)
                g = (spread[:, j * 128 : j * 128 + 128] * slope).astype(BF)
                wide = g.astype(F32)
                if d < 4 and j < 4:
                    deep_sum = deep_sum + wide
                moved = jnp.where(lane < 127, pltpu.roll(wide, 127, 1), 0.0).astype(BF)
                for sd in range(2):
                    for sh in range(2):
                        if 0 <= d - sd < 4 and 0 <= j - sh < 4:
                            at = cell(s, d - sd, j - sh)
                            r = (sd * 4 + sh * 2) * 32
                            g_buf[r : r + 32, at] = g
                            g_buf[r + 32 : r + 64, at] = moved

    z = iota((256, 512), 0)
    col = iota((256, 512), 1)
    shifts = jnp.where(z == 2 * (col & 127) + (col >> 7) - 1, 1.0, 0.0).astype(BF)
    row = iota((160, 256), 0)
    high = 8 * me + (row >> 4) - 1
    target = ((row >> 2) & 3) * 64 + (high >> 3) * 32 + (row & 3) * 8 + (high & 7)
    lift = one_hot(jnp.where((high >= 0) & (high < 16), target, -1), (160, 256))
    for s in range(2):
        for d in range(10):
            x = jnp.concatenate(
                [img[half, s, :, d].astype(F32).reshape(32, 256) for half in range(2)], axis=0
            ).astype(BF)
            y = dot(x, shifts).astype(BF)
            y = jnp.concatenate([y[:, o * 128 : o * 128 + 128] for o in range(4)], axis=0)
            t = dot(lift, y).astype(BF)
            for hh in range(10):
                for od in range(4):
                    for oh in range(4):
                        if (d - od) % 2 == 0 and (hh - oh) % 2 == 0:
                            d2, h2 = (d - od) // 2, (hh - oh) // 2
                            if 0 <= d2 < 4 and 0 <= h2 < 4:
                                r = (od * 4 + oh) * 16
                                i_buf[r : r + 16, cell(s, d2, h2)] = t[hh * 16 : hh * 16 + 16]

    taps = {}
    for a in range(3):
        for b in range(3):
            for c in range(3):
                (sd, pd_), (sh, ph), (sw, pw) = TAP[a], TAP[b], TAP[c]
                taps[(pd_, pw, ph, sd, sh, sw)] = a * 9 + b * 3 + c
    bands = []
    zero = jnp.zeros((16, 32), F32)
    for p in range(8):
        phase = (p // 4, (p // 2) % 2, p % 2)
        pieces = []
        for s in range(8):
            t = taps.get(phase + (s // 4, (s // 2) % 2, s % 2))
            pieces.append(zero if t is None else weight[t].astype(F32))
        bands.append(jnp.concatenate(pieces, axis=1))
    matrix = jnp.concatenate(bands, axis=0).astype(BF)

    deep = jnp.zeros((128, 256), F32)
    first = jnp.zeros((128, 256), F32)
    first_sum = jnp.zeros((128, 128), F32)
    step = 512
    for at in range(0, 4096, step):
        part = slice(at, at + step)
        g = g_buf[:, part]
        pre = ph_buf[:, part].astype(F32)
        grad = dot(matrix, g).astype(BF).astype(F32)
        grad = (grad * jnp.where(pre > 0, 1.0, SLOPE)).astype(BF)
        act = jnp.where(pre > 0, pre, SLOPE * pre).astype(BF)
        wide = grad.astype(F32)
        for o in range(0, step, 128):
            first_sum = first_sum + wide[:, o : o + 128]
        deep = deep + dot_nt(act, g)
        first = first + dot_nt(grad, i_buf[:, part])

    order = sorted((t, key) for key, t in taps.items())
    blocks = []
    for t, (pd_, pw, ph, sd, sh, sw) in order:
        r = (pd_ * 4 + pw * 2 + ph) * 16
        c = (sd * 4 + sh * 2 + sw) * 32
        blocks.append(deep[r : r + 16, c : c + 32])
    blocks += [zero] * 5
    for q in range(4):
        out[q * 16 : q * 16 + 16, :] = jnp.concatenate(blocks[q * 8 : q * 8 + 8], axis=1)
    total = jnp.zeros((16, 256), F32)
    bias = jnp.sum(first_sum, axis=1, keepdims=True)
    first_bias = jnp.zeros((16, 1), F32)
    for p in range(8):
        pd_, pw, ph = p // 4, (p // 2) % 2, p % 2
        move = pd_ * 64 + ph * 16 + pw * 4
        piece = first[p * 16 : p * 16 + 16]
        total = total + (pltpu.roll(piece, 256 - move, 1) if move else piece)
        first_bias = first_bias + bias[p * 16 : p * 16 + 16]
    deep_bias = jnp.sum(deep_sum, axis=1, keepdims=True)
    lane = iota((16, 256), 1)
    total = jnp.where(lane == 12, first_bias, total)
    total = jnp.where(lane == 13, deep_bias[0:16], total)
    total = jnp.where(lane == 14, deep_bias[16:32], total)
    out[64:80, :] = total
    if out.shape[0] > 80:
        out[80:, :] = jnp.zeros((out.shape[0] - 80, 256), F32)


def compute(rows, hidden, img_all, pd_all, pool_all, weight):
    return pl.pallas_call(
        compute_kernel,
        out_shape=jax.ShapeDtypeStruct((rows, 256), F32),
        in_specs=[vmem()] * 5,
        out_specs=vmem(),
        scratch_shapes=[
            pltpu.VMEM((128, 4096), BF),
            pltpu.VMEM((256, 4096), BF),
            pltpu.VMEM((256, 4096), BF),
        ],
    )(hidden, img_all, pd_all, pool_all, weight)


def reduce_kernel(members, heights, src, whole, arrived, mine, sems):
    me = lax.axis_index("depth") * heights + lax.axis_index("height")
    size = src.shape[0] // members
    barrier = pltpu.get_barrier_semaphore()

    def device(index):
        return {"depth": index // heights, "height": index % heights}

    peers = [lax.rem(me + j, members) for j in range(members)]
    for j in range(1, members):
        pl.semaphore_signal(barrier, inc=1, device_id=device(peers[j]), device_id_type=MESH)
    pl.semaphore_wait(barrier, members - 1)

    def block(index):
        return pl.ds(pl.multiple_of(index * size, 8), size)

    scatter = []
    for j in range(1, members):
        scatter.append(
            pltpu.make_async_remote_copy(
                src_ref=src.at[block(peers[j])],
                dst_ref=arrived.at[j],
                send_sem=sems.at[0, j],
                recv_sem=sems.at[1, j],
                device_id=device(peers[j]),
                device_id_type=MESH,
            )
        )
    for c in scatter:
        c.start()
    total = src[block(me), :]
    for j, c in enumerate(scatter):
        c.wait_recv()
        total = total + arrived[j + 1]
    mine[...] = total
    whole[block(me), :] = total
    gather = []
    for j in range(1, members):
        gather.append(
            pltpu.make_async_remote_copy(
                src_ref=mine,
                dst_ref=whole.at[block(me)],
                send_sem=sems.at[2, j],
                recv_sem=sems.at[3, j],
                device_id=device(peers[j]),
                device_id_type=MESH,
            )
        )
    for c in gather:
        c.start()
    for c in scatter:
        c.wait_send()
    for j in range(1, members):
        source = lax.rem(me + members - j, members)
        pltpu.make_async_remote_copy(
            src_ref=mine,
            dst_ref=whole.at[block(source)],
            send_sem=sems.at[2, j],
            recv_sem=sems.at[3, j],
            device_id=device(source),
            device_id_type=MESH,
        ).wait_recv()
    for c in gather:
        c.wait_send()


def unpack_kernel(whole, deep, first, deep_bias, first_bias):
    for t in range(27):
        r, c = (t // 8) * 16, (t % 8) * 32
        deep[t] = whole[r : r + 16, c : c + 32]
    flipped = jnp.transpose(whole[64:80, :])
    for t in range(27):
        r = (t // 9) * 64 + ((t // 3) % 3) * 16 + (t % 3) * 4
        first[t] = flipped[r : r + 4]
    first_bias[...] = flipped[12:13]
    deep_bias[...] = jnp.concatenate([flipped[13:14], flipped[14:15]], axis=1)


def reduce_all(members, heights, packed):
    size = packed.shape[0] // members
    return pl.pallas_call(
        functools.partial(reduce_kernel, members, heights),
        out_shape=jax.ShapeDtypeStruct(packed.shape, F32),
        in_specs=[vmem()],
        out_specs=vmem(),
        scratch_shapes=[
            pltpu.VMEM((members, size, 256), F32),
            pltpu.VMEM((size, 256), F32),
            pltpu.SemaphoreType.DMA((4, members)),
        ],
        compiler_params=pltpu.CompilerParams(collective_id=1, has_side_effects=True),
    )(packed)


def unpack(whole):
    return pl.pallas_call(
        unpack_kernel,
        out_shape=(
            jax.ShapeDtypeStruct((27, 16, 32), F32),
            jax.ShapeDtypeStruct((27, 4, 16), F32),
            jax.ShapeDtypeStruct((1, 32), F32),
            jax.ShapeDtypeStruct((1, 16), F32),
        ),
        in_specs=[vmem()],
        out_specs=(vmem(),) * 4,
    )(whole)


def on_device(count, heights, images, pre_hidden, pre_deep, pooled_grad, deep_weight):
    img_all, pd_all, pool_all = exchange(count, images, pre_deep[0], pooled_grad[0])
    weight = deep_weight.transpose(2, 3, 4, 1, 0).reshape(27, 16, 32)
    members = count * heights
    size = 8 * (-(-80 // (8 * members)))
    packed = compute(members * size, pre_hidden, img_all, pd_all, pool_all, weight)
    deep, first, deep_bias, first_bias = unpack(reduce_all(members, heights, packed))
    return (
        first.reshape(3, 3, 3, 4, 16).transpose(4, 3, 0, 1, 2),
        first_bias.reshape(16),
        deep.reshape(3, 3, 3, 16, 32).transpose(4, 3, 0, 1, 2),
        deep_bias.reshape(32),
    )


def solution(mesh):
    return jax.shard_map(
        functools.partial(on_device, mesh.shape["depth"], mesh.shape["height"]),
        mesh=mesh,
        in_specs=(
            P("groups", None, "depth", "height", None),
            P("groups", None, "depth", "height", None),
            P(("groups", "height"), None, "depth", None, None),
            P(("groups", "height"), None, "depth", None),
            P(),
        ),
        out_specs=(
            P("groups", None, None, None, None),
            P("groups"),
            P("groups", None, None, None, None),
            P("groups"),
        ),
        check_vma=False,
    )
```

```python
import functools

import jax
import jax.numpy as jnp
from jax import lax
from jax.experimental import pallas as pl
from jax.experimental.pallas import tpu as pltpu
from jax.sharding import PartitionSpec as P

SLOPE = 0.3
MESH = pl.DeviceIdType.MESH
BF = jnp.bfloat16
F32 = jnp.float32
TAP = ((1, 1), (0, 0), (0, 1))


def vmem():
    return pl.BlockSpec(memory_space=pltpu.VMEM)


def iota(shape, dim):
    return lax.broadcasted_iota(jnp.int32, shape, dim)


def one_hot(row_target, shape):
    return jnp.where(row_target == iota(shape, 1), 1.0, 0.0).astype(BF)


def dot(a, b):
    return jnp.dot(a, b, preferred_element_type=F32)


def dot_nt(a, b):
    return lax.dot_general(a, b, (((1,), (1,)), ((), ())), preferred_element_type=F32)


def fused_kernel(
    count, heights, hid, img, pd, pool, weight, whole,
    img_all, pd_all, pool_all, ph_buf, g_buf, i_buf, src, arrived, mine, send, recv, sems,
):
    k = lax.axis_index("depth")
    h = lax.axis_index("height")
    members = count * heights
    index = k * heights + h
    cells = img.shape[2]
    quarter = pd.shape[1]

    def device(number):
        return {"depth": number // heights, "height": number % heights}

    peers = [lax.rem(index + j, members) for j in range(members)]
    barrier = pltpu.get_barrier_semaphore()
    for j in range(1, members):
        pl.semaphore_signal(barrier, inc=1, device_id=device(peers[j]), device_id_type=MESH)

    def cell(s, d2, h2):
        at = ((s * 4 + d2) * 4 + h2) * 128
        return slice(at, at + 128)

    row = iota((128, 128), 0)
    order = one_hot((row & 15) * 8 + (row >> 4), (128, 128))
    z = iota((256, 256), 0)
    col = iota((256, 256), 1)
    split = jnp.where(z == 2 * (col & 127) + (col >> 7), 1.0, 0.0).astype(BF)

    def hidden_rows(s, d):
        x = hid[s, :, d].astype(F32).reshape(128, 256).astype(BF)
        a = dot(x, split).astype(BF)
        b = dot(order, a).astype(BF)
        for h2 in range(4):
            for pw in range(2):
                r = (d % 2) * 64 + pw * 32
                ph_buf[r : r + 32, cell(s, d // 2, h2)] = b[
                    h2 * 32 : h2 * 32 + 32, pw * 128 : pw * 128 + 128
                ]

    for s in range(2):
        for d in range(8):
            hidden_rows(s, d)

    pl.semaphore_wait(barrier, members - 1)

    def copy(src_ref, dst_ref, slot, depth, height):
        return pltpu.make_async_remote_copy(
            src_ref=src_ref,
            dst_ref=dst_ref,
            send_sem=send.at[slot],
            recv_sem=recv.at[slot],
            device_id={"depth": depth, "height": height},
            device_id_type=MESH,
        )

    def partner(slot):
        return [
            copy(pd, pd_all.at[slot, :, 0:quarter], 0, k, 1 - h),
            copy(pool, pool_all.at[slot, 0], 1, k, 1 - h),
            copy(img, img_all.at[slot, :, :, 1 : cells + 1], 2, k, 1 - h),
        ]

    def down():
        return [
            copy(pd.at[:, 0:1], pd_all.at[h, :, quarter : quarter + 1], 3, k - 1, h),
            copy(pool, pool_all.at[h, 1], 4, k - 1, h),
            copy(img.at[:, :, 0:1], img_all.at[h, :, :, cells + 1 : cells + 2], 5, k - 1, h),
        ]

    def up():
        return [copy(img.at[:, :, cells - 1 : cells], img_all.at[h, :, :, 0:1], 6, k + 1, h)]

    def relay_above(slot):
        parts = [
            pd_all.at[slot, :, quarter : quarter + 1],
            pool_all.at[slot, 1],
            img_all.at[slot, :, :, cells + 1 : cells + 2],
        ]
        return [copy(p, p, 7 + n, k, 1 - h) for n, p in enumerate(parts)]

    def relay_below(slot):
        part = img_all.at[slot, :, :, 0:1]
        return [copy(part, part, 10, k, 1 - h)]

    @pl.when(k > 0)
    def _():
        for c in down():
            c.start()

    @pl.when(k < count - 1)
    def _():
        for c in up():
            c.start()

    for c in partner(h):
        c.start()
    img_all[h, :, :, 1 : cells + 1] = img[...]
    pd_all[h, :, 0:quarter] = pd[...]
    pool_all[h, 0] = pool[...]

    @pl.when(k == 0)
    def _():
        img_all[:, :, :, 0:1] = jnp.zeros_like(img_all[:, :, :, 0:1])

    @pl.when(k == count - 1)
    def _():
        img_all[:, :, :, cells + 1 : cells + 2] = jnp.zeros_like(img_all[:, :, :, 0:1])
        pd_all[:, :, quarter : quarter + 1] = jnp.zeros_like(pd_all[:, :, 0:1])
        pool_all[:, 1] = jnp.zeros_like(pool_all[:, 1])

    taps = {}
    for a in range(3):
        for b in range(3):
            for c in range(3):
                (sd, pd_), (sh, ph), (sw, pw) = TAP[a], TAP[b], TAP[c]
                taps[(pd_, pw, ph, sd, sh, sw)] = a * 9 + b * 3 + c
    bands = []
    zero = jnp.zeros((16, 32), F32)
    for p in range(8):
        phase = (p // 4, (p // 2) % 2, p % 2)
        pieces = []
        for s in range(8):
            t = taps.get(phase + (s // 4, (s // 2) % 2, s % 2))
            pieces.append(zero if t is None else weight[t].astype(F32))
        bands.append(jnp.concatenate(pieces, axis=1))
    matrix = jnp.concatenate(bands, axis=0).astype(BF)

    row = iota((160, 256), 0)
    high = 4 * h + (row >> 5)
    pick = one_hot(jnp.where(high < 8, (row & 31) * 8 + high, -1), (160, 256))
    r640 = iota((256, 640), 0)
    c640 = iota((256, 640), 1)
    spread_mat = jnp.where(
        r640 == ((4 * h + (c640 >> 7)) >> 1) * 64 + ((c640 & 127) >> 1), 1.0, 0.0
    ).astype(BF)
    z = iota((256, 512), 0)
    col = iota((256, 512), 1)
    shifts = jnp.where(z == 2 * (col & 127) + (col >> 7) - 1, 1.0, 0.0).astype(BF)
    high = 8 * h + (row >> 4) - 1
    target = ((row >> 2) & 3) * 64 + (high >> 3) * 32 + (row & 3) * 8 + (high & 7)
    lift = one_hot(jnp.where((high >= 0) & (high < 16), target, -1), (160, 256))
    lane = iota((32, 128), 1)

    for c in partner(1 - h):
        c.wait_recv()

    sums = {"deep": jnp.zeros((32, 128), F32)}

    def gradient_rows(s, depths):
        coarse = pool_all[s, depths[0] // 4].astype(F32)
        spread = dot(coarse[:, (depths[0] // 2) % 2, :].astype(BF), spread_mat) / 8.0
        for d in depths:
            x = pd_all[s, :, d].astype(F32).reshape(256, 128).astype(BF)
            y = dot(pick, x)
            for j in range(5):
                slope = jnp.where(y[j * 32 : j * 32 + 32] > 0, 1.0, SLOPE)
                g = (spread[:, j * 128 : j * 128 + 128] * slope).astype(BF)
                wide = g.astype(F32)
                if d < 4 and j < 4:
                    sums["deep"] = sums["deep"] + wide
                moved = jnp.where(lane < 127, pltpu.roll(wide, 127, 1), 0.0).astype(BF)
                for sd in range(2):
                    for sh in range(2):
                        if 0 <= d - sd < 4 and 0 <= j - sh < 4:
                            at = cell(s, d - sd, j - sh)
                            r = (sd * 4 + sh * 2) * 32
                            g_buf[r : r + 32, at] = g
                            g_buf[r + 32 : r + 64, at] = moved

    def image_rows(s, d):
        x = jnp.concatenate(
            [img_all[half, s, :, d].astype(F32).reshape(32, 256) for half in range(2)], axis=0
        ).astype(BF)
        y = dot(x, shifts).astype(BF)
        y = jnp.concatenate([y[:, o * 128 : o * 128 + 128] for o in range(4)], axis=0)
        t = dot(lift, y).astype(BF)
        for hh in range(10):
            for od in range(4):
                for oh in range(4):
                    if (d - od) % 2 == 0 and (hh - oh) % 2 == 0:
                        d2, h2 = (d - od) // 2, (hh - oh) // 2
                        if 0 <= d2 < 4 and 0 <= h2 < 4:
                            r = (od * 4 + oh) * 16
                            i_buf[r : r + 16, cell(s, d2, h2)] = t[hh * 16 : hh * 16 + 16]

    sums["kernel"] = jnp.zeros((128, 256), F32)
    sums["first"] = jnp.zeros((128, 256), F32)
    sums["bias"] = jnp.zeros((128, 128), F32)

    def contract(s, d2):
        at = (s * 4 + d2) * 512
        part = slice(at, at + 512)
        g = g_buf[:, part]
        pre = ph_buf[:, part].astype(F32)
        grad = dot(matrix, g).astype(BF).astype(F32)
        grad = (grad * jnp.where(pre > 0, 1.0, SLOPE)).astype(BF)
        act = jnp.where(pre > 0, pre, SLOPE * pre).astype(BF)
        wide = grad.astype(F32)
        for o in range(0, 512, 128):
            sums["bias"] = sums["bias"] + wide[:, o : o + 128]
        sums["kernel"] = sums["kernel"] + dot_nt(act, g)
        sums["first"] = sums["first"] + dot_nt(grad, i_buf[:, part])

    for s in range(2):
        gradient_rows(s, (0, 1))
        gradient_rows(s, (2, 3))
        for d in range(1, 9):
            image_rows(s, d)

    @pl.when(k < count - 1)
    def _():
        for c, r in zip(down(), relay_above(h)):
            c.wait_recv()
            r.start()

    @pl.when(k > 0)
    def _():
        for c, r in zip(up(), relay_below(h)):
            c.wait_recv()
            r.start()

    for s in range(2):
        contract(s, 1)
        contract(s, 2)

    @pl.when(k < count - 1)
    def _():
        for c in relay_above(1 - h):
            c.wait_recv()

    @pl.when(k > 0)
    def _():
        for c in relay_below(1 - h):
            c.wait_recv()

    for s in range(2):
        gradient_rows(s, (4,))
        image_rows(s, 0)
        image_rows(s, 9)
        contract(s, 0)
        contract(s, 3)

    deep, first = sums["kernel"], sums["first"]
    blocks = []
    for t, (pd_, pw, ph, sd, sh, sw) in sorted((t, key) for key, t in taps.items()):
        r = (pd_ * 4 + pw * 2 + ph) * 16
        c = (sd * 4 + sh * 2 + sw) * 32
        blocks.append(deep[r : r + 16, c : c + 32])
    total = jnp.zeros((16, 256), F32)
    bias = jnp.sum(sums["bias"], axis=1, keepdims=True)
    first_bias = jnp.zeros((16, 1), F32)
    for p in range(8):
        pd_, pw, ph = p // 4, (p // 2) % 2, p % 2
        move = pd_ * 64 + ph * 16 + pw * 4
        piece = first[p * 16 : p * 16 + 16]
        total = total + (pltpu.roll(piece, 256 - move, 1) if move else piece)
        first_bias = first_bias + bias[p * 16 : p * 16 + 16]
    deep_bias = jnp.sum(sums["deep"], axis=1, keepdims=True)
    lane = iota((16, 256), 1)
    total = jnp.where(lane == 12, first_bias, total)
    total = jnp.where(lane == 13, deep_bias[0:16], total)
    total = jnp.where(lane == 14, deep_bias[16:32], total)
    blocks.append(jnp.concatenate([total[:, 160:176], jnp.zeros((16, 16), F32)], axis=1))
    for q in range(7):
        src[q * 16 : q * 16 + 16, :] = jnp.concatenate(blocks[q * 4 : q * 4 + 4], axis=1)
    src[112:128, :] = jnp.concatenate([total[:, 0:48], total[:, 64:112], total[:, 128:160]], axis=1)
    if src.shape[0] > 128:
        src[128:, :] = jnp.zeros((src.shape[0] - 128, 128), F32)

    size = src.shape[0] // members

    def block(number):
        return pl.ds(pl.multiple_of(number * size, 8), size)

    def hop(src_ref, dst_ref, phase, j, number):
        return pltpu.make_async_remote_copy(
            src_ref=src_ref,
            dst_ref=dst_ref,
            send_sem=sems.at[2 * phase, j],
            recv_sem=sems.at[2 * phase + 1, j],
            device_id=device(number),
            device_id_type=MESH,
        )

    scatter = [hop(src.at[block(peers[j])], arrived.at[j], 0, j, peers[j]) for j in range(1, members)]
    for c in scatter:
        c.start()
    total = src[block(index), :]
    for j, c in enumerate(scatter):
        c.wait_recv()
        total = total + arrived[j + 1]
    mine[...] = total
    whole[block(index), :] = total
    gather = [hop(mine, whole.at[block(index)], 1, j, peers[j]) for j in range(1, members)]
    for c in gather:
        c.start()

    for c in scatter + partner(h):
        c.wait_send()

    @pl.when(k > 0)
    def _():
        for c in down() + relay_below(h):
            c.wait_send()

    @pl.when(k < count - 1)
    def _():
        for c in up() + relay_above(h):
            c.wait_send()

    for j in range(1, members):
        source = lax.rem(index + members - j, members)
        hop(mine, whole.at[block(source)], 1, j, source).wait_recv()
    for c in gather:
        c.wait_send()


def fused(count, heights, hidden, images, pre_deep, pooled, weight):
    samples, chans, cells, rows, width = images.shape
    out_chans, coarse, coarse_rows, coarse_width = pre_deep.shape
    members = count * heights
    size = 8 * (-(-128 // (8 * members)))
    return pl.pallas_call(
        functools.partial(fused_kernel, count, heights),
        out_shape=jax.ShapeDtypeStruct((members * size, 128), F32),
        in_specs=[vmem()] * 5,
        out_specs=vmem(),
        scratch_shapes=[
            pltpu.VMEM((2, samples, chans, cells + 2, rows, width), BF),
            pltpu.VMEM((2, out_chans, coarse + 1, coarse_rows, coarse_width), BF),
            pltpu.VMEM((2, 2) + pooled.shape, BF),
            pltpu.VMEM((128, 4096), BF),
            pltpu.VMEM((256, 4096), BF),
            pltpu.VMEM((256, 4096), BF),
            pltpu.VMEM((members * size, 128), F32),
            pltpu.VMEM((members, size, 128), F32),
            pltpu.VMEM((size, 128), F32),
            pltpu.SemaphoreType.DMA((11,)),
            pltpu.SemaphoreType.DMA((11,)),
            pltpu.SemaphoreType.DMA((4, members)),
        ],
        compiler_params=pltpu.CompilerParams(collective_id=0, has_side_effects=True),
    )(hidden, images, pre_deep, pooled, weight)


def unpack_kernel(whole, deep, first, deep_bias, first_bias):
    for t in range(27):
        r, c = (t // 4) * 16, (t % 4) * 32
        deep[t] = whole[r : r + 16, c : c + 32]
    flipped = jnp.transpose(whole[112:128, :])
    rest = jnp.transpose(whole[96:112, :])[96:112]
    for t in range(27):
        r = (t // 9) * 48 + ((t // 3) % 3) * 16 + (t % 3) * 4
        first[t] = flipped[r : r + 4] if r < 128 else rest[r - 128 : r - 124]
    first_bias[...] = flipped[12:13]
    deep_bias[...] = jnp.concatenate([flipped[13:14], flipped[14:15]], axis=1)


def unpack(whole):
    return pl.pallas_call(
        unpack_kernel,
        out_shape=(
            jax.ShapeDtypeStruct((27, 16, 32), F32),
            jax.ShapeDtypeStruct((27, 4, 16), F32),
            jax.ShapeDtypeStruct((1, 32), F32),
            jax.ShapeDtypeStruct((1, 16), F32),
        ),
        in_specs=[vmem()],
        out_specs=(vmem(),) * 4,
    )(whole)


def on_device(count, heights, images, pre_hidden, pre_deep, pooled_grad, deep_weight):
    weight = deep_weight.transpose(2, 3, 4, 1, 0).reshape(27, 16, 32)
    whole = fused(count, heights, pre_hidden, images, pre_deep[0], pooled_grad[0], weight)
    deep, first, deep_bias, first_bias = unpack(whole)
    return (
        first.reshape(3, 3, 3, 4, 16).transpose(4, 3, 0, 1, 2),
        first_bias.reshape(16),
        deep.reshape(3, 3, 3, 16, 32).transpose(4, 3, 0, 1, 2),
        deep_bias.reshape(32),
    )


def solution(mesh):
    return jax.shard_map(
        functools.partial(on_device, mesh.shape["depth"], mesh.shape["height"]),
        mesh=mesh,
        in_specs=(
            P("groups", None, "depth", "height", None),
            P("groups", None, "depth", "height", None),
            P(("groups", "height"), None, "depth", None, None),
            P(("groups", "height"), None, "depth", None),
            P(),
        ),
        out_specs=(
            P("groups", None, None, None, None),
            P("groups"),
            P("groups", None, None, None, None),
            P("groups"),
        ),
        check_vma=False,
    )
```

```python
import functools

import jax
import jax.numpy as jnp
from jax import lax
from jax.experimental import pallas as pl
from jax.experimental.pallas import tpu as pltpu
from jax.sharding import PartitionSpec as P

SLOPE = 0.3
MESH = pl.DeviceIdType.MESH
BF = jnp.bfloat16
F32 = jnp.float32
TAP = ((1, 1), (0, 0), (0, 1))


def vmem():
    return pl.BlockSpec(memory_space=pltpu.VMEM)


def iota(shape, dim):
    return lax.broadcasted_iota(jnp.int32, shape, dim)


def one_hot(row_target, shape):
    return jnp.where(row_target == iota(shape, 1), 1.0, 0.0).astype(BF)


def dot(a, b):
    return jnp.dot(a, b, preferred_element_type=F32)


def dot_nt(a, b):
    return lax.dot_general(a, b, (((1,), (1,)), ((), ())), preferred_element_type=F32)


def fused_kernel(
    count, heights, hid_in, img_in, pd_in, pool_in, weight_in, whole,
    hid, weight, img_all, pd_all, pool_all, ph_buf, f_buf, g_buf, y_buf, i_buf, src, arrived, mine,
    local, send, recv, sems,
):
    k = lax.axis_index("depth")
    h = lax.axis_index("height")
    members = count * heights
    index = k * heights + h
    cells = img_in.shape[2]
    quarter = pd_in.shape[1]

    def device(number):
        return {"depth": number // heights, "height": number % heights}

    def flipped(j):
        if members & (members - 1):
            return lax.rem(index + j, members)
        total, bit = 0, 1
        while bit < members:
            digit = (index // bit) % 2
            total = total + bit * (1 - digit if j & bit else digit)
            bit *= 2
        return total

    def origin(j):
        if members & (members - 1):
            return lax.rem(index + members - j, members)
        return flipped(j)

    turns = list(range(members - 1, 0, -1))
    peers = {j: flipped(j) for j in turns}
    barrier = pltpu.get_barrier_semaphore()
    for j in turns:
        pl.semaphore_signal(barrier, inc=1, device_id=device(peers[j]), device_id_type=MESH)

    loads = [
        pltpu.make_async_copy(hid_in, hid, local.at[0]),
        pltpu.make_async_copy(pd_in, pd_all.at[h, :, 0:quarter], local.at[1]),
        pltpu.make_async_copy(pool_in, pool_all.at[h, 0], local.at[2]),
        pltpu.make_async_copy(img_in, img_all.at[h, :, :, 1 : cells + 1], local.at[3]),
        pltpu.make_async_copy(weight_in, weight, local.at[4]),
    ]
    for c in loads:
        c.start()

    row = iota((128, 128), 0)
    order = one_hot((row & 15) * 8 + (row >> 4), (128, 128))
    z = iota((256, 256), 0)
    col = iota((256, 256), 1)
    split = jnp.where(z == 2 * (col & 127) + (col >> 7), 1.0, 0.0).astype(BF)

    def hidden_rows(s, d):
        x = hid[s, :, d].astype(F32).reshape(128, 256).astype(BF)
        a = dot(x, split).astype(BF)
        b = dot(order, a).astype(BF)
        for h2 in range(4):
            for pw in range(2):
                r = (d % 2) * 64 + pw * 32
                at = (d // 2) * 1024 + s * 512 + h2 * 128
                ph_buf[r : r + 32, at : at + 128] = b[
                    h2 * 32 : h2 * 32 + 32, pw * 128 : pw * 128 + 128
                ]

    loads[0].wait()
    for s in range(2):
        for d in range(8):
            hidden_rows(s, d)

    row = iota((160, 256), 0)
    high = 4 * h + (row >> 5)
    pick = one_hot(jnp.where(high < 8, (row & 31) * 8 + high, -1), (160, 256))
    r640 = iota((256, 640), 0)
    c640 = iota((256, 640), 1)
    spread_mat = jnp.where(
        r640 == ((4 * h + (c640 >> 7)) >> 1) * 64 + ((c640 & 127) >> 1), 1.0, 0.0
    ).astype(BF)
    z = iota((256, 512), 0)
    col = iota((256, 512), 1)
    shifts = jnp.where(z == 2 * (col & 127) + (col >> 7) - 1, 1.0, 0.0).astype(BF)
    high = 8 * h + (row >> 4) - 1
    target = ((row >> 2) & 3) * 64 + (high >> 3) * 32 + (row & 3) * 8 + (high & 7)
    lift = one_hot(jnp.where((high >= 0) & (high < 16), target, -1), (160, 256))
    lane = iota((32, 128), 1)
    for c in loads[1:]:
        c.wait()

    pl.semaphore_wait(barrier, members - 1)

    def copy(src_ref, dst_ref, slot, depth, height):
        return pltpu.make_async_remote_copy(
            src_ref=src_ref,
            dst_ref=dst_ref,
            send_sem=send.at[slot],
            recv_sem=recv.at[slot],
            device_id={"depth": depth, "height": height},
            device_id_type=MESH,
        )

    def same(part, slot):
        return copy(part, part, slot, k, 1 - h)

    def partner(slot):
        return [
            same(pd_all.at[slot, :, 0:quarter], 0),
            same(pool_all.at[slot, 0], 1),
            same(img_all.at[slot, :, :, 1 : cells + 1], 2),
        ]

    def down():
        return [
            copy(pd_all.at[h, :, 0:1], pd_all.at[h, :, quarter : quarter + 1], 3, k - 1, h),
            copy(pool_all.at[h, 0], pool_all.at[h, 1], 4, k - 1, h),
            copy(img_all.at[h, :, :, 1:2], img_all.at[h, :, :, cells + 1 : cells + 2], 5, k - 1, h),
        ]

    def up():
        return [copy(img_all.at[h, :, :, cells : cells + 1], img_all.at[h, :, :, 0:1], 6, k + 1, h)]

    def relay_above(slot):
        return [
            same(pd_all.at[slot, :, quarter : quarter + 1], 7),
            same(pool_all.at[slot, 1], 8),
            same(img_all.at[slot, :, :, cells + 1 : cells + 2], 9),
        ]

    def relay_below(slot):
        return [same(img_all.at[slot, :, :, 0:1], 10)]

    @pl.when(k > 0)
    def _():
        for c in down():
            c.start()

    @pl.when(k < count - 1)
    def _():
        for c in up():
            c.start()

    for c in partner(h):
        c.start()

    @pl.when(k == 0)
    def _():
        img_all[:, :, :, 0:1] = jnp.zeros_like(img_all[:, :, :, 0:1])

    @pl.when(k == count - 1)
    def _():
        img_all[:, :, :, cells + 1 : cells + 2] = jnp.zeros_like(img_all[:, :, :, 0:1])
        pd_all[:, :, quarter : quarter + 1] = jnp.zeros_like(pd_all[:, :, 0:1])
        pool_all[:, 1] = jnp.zeros_like(pool_all[:, 1])

    taps = {}
    for a in range(3):
        for b in range(3):
            for c in range(3):
                (sd, pd_), (sh, ph), (sw, pw) = TAP[a], TAP[b], TAP[c]
                taps[(pd_, pw, ph, sd, sh, sw)] = a * 9 + b * 3 + c
    bands = []
    zero = jnp.zeros((16, 32), F32)
    for p in range(8):
        phase = (p // 4, (p // 2) % 2, p % 2)
        pieces = []
        for s in range(8):
            t = taps.get(phase + (s // 4, (s // 2) % 2, s % 2))
            pieces.append(zero if t is None else weight[t].astype(F32))
        bands.append(jnp.concatenate(pieces, axis=1))
    matrix = jnp.concatenate(bands, axis=0).astype(BF)

    sums = {"deep": jnp.zeros((32, 128), F32)}

    def gradient_rows(s, depths):
        x = jnp.concatenate(
            [pd_all[s, :, d].astype(F32).reshape(256, 128).astype(BF) for d in depths], axis=1
        )
        y = dot(pick, x)
        coarse = pool_all[s, depths[0] // 4].astype(F32)
        halves = sorted({(d // 2) % 2 for d in depths})
        rows = jnp.concatenate([coarse[:, n, :] for n in halves], axis=0).astype(BF)
        spread = dot(rows, spread_mat) / 8.0
        for n, d in enumerate(depths):
            r = halves.index((d // 2) % 2) * 32
            for j in range(5):
                pre = y[j * 32 : j * 32 + 32, n * 128 : n * 128 + 128]
                slope = jnp.where(pre > 0, 1.0, SLOPE)
                g = (spread[r : r + 32, j * 128 : j * 128 + 128] * slope).astype(BF)
                wide = g.astype(F32)
                if d < 4 and j < 4:
                    sums["deep"] = sums["deep"] + wide
                moved = jnp.where(lane < 127, pltpu.roll(wide, 127, 1), 0.0).astype(BF)
                for sd in range(2):
                    for sh in range(2):
                        if 0 <= d - sd < 4 and 0 <= j - sh < 4:
                            at = pl.multiple_of((d - sd) * 1024 + s * 512 + (j - sh) * 128, 128)
                            r2 = (sd * 4 + sh * 2) * 32
                            g_buf[r2 : r2 + 32, pl.ds(at, 128)] = g
                            g_buf[r2 + 32 : r2 + 64, pl.ds(at, 128)] = moved

    def image_shift(half, depths):
        x = jnp.concatenate(
            [img_all[half, s, :, d].astype(F32).reshape(32, 256) for d in depths for s in range(2)], axis=0
        ).astype(BF)
        y = dot(x, shifts).astype(BF)
        for n, d in enumerate(depths):
            for s in range(2):
                r = (n * 2 + s) * 32
                at = (d * 2 + s) * 128
                for o in range(4):
                    low = pl.multiple_of(o * 64 + half * 32, 32)
                    y_buf[pl.ds(low, 32), at : at + 128] = y[r : r + 32, o * 128 : o * 128 + 128]

    def image_rows(first_depth, depths):
        at = first_depth * 256
        t = dot(lift, y_buf[:, at : at + 256 * depths]).astype(BF)
        for d in range(first_depth, first_depth + depths):
            for hh in range(10):
                for od in range(4):
                    for oh in range(4):
                        if (d - od) % 2 == 0 and (hh - oh) % 2 == 0:
                            d2, h2 = (d - od) // 2, (hh - oh) // 2
                            if 0 <= d2 < 4 and 0 <= h2 < 4:
                                r = (od * 4 + oh) * 16
                                for s in range(2):
                                    to = d2 * 1024 + s * 512 + h2 * 128
                                    c = ((d - first_depth) * 2 + s) * 128
                                    i_buf[r : r + 16, to : to + 128] = t[
                                        hh * 16 : hh * 16 + 16, c : c + 128
                                    ]

    sums["kernel"] = jnp.zeros((128, 256), F32)
    sums["first"] = jnp.zeros((128, 256), F32)
    sums["bias"] = jnp.zeros((128, 128), F32)

    def contract(d2, blocks):
        for at in range(d2 * 1024, (d2 + blocks) * 1024, 512):
            part = slice(at, at + 512)
            pre = ph_buf[:, part].astype(F32)
            grad = dot(matrix, g_buf[:, part]).astype(BF).astype(F32)
            grad = (grad * jnp.where(pre > 0, 1.0, SLOPE)).astype(BF)
            ph_buf[:, part] = jnp.where(pre > 0, pre, SLOPE * pre).astype(BF)
            f_buf[:, part] = grad
            wide = grad.astype(F32)
            for o in range(0, 512, 128):
                sums["bias"] = sums["bias"] + wide[:, o : o + 128]
        part = slice(d2 * 1024, (d2 + blocks) * 1024)
        sums["kernel"] = sums["kernel"] + dot_nt(ph_buf[:, part], g_buf[:, part])
        sums["first"] = sums["first"] + dot_nt(f_buf[:, part], i_buf[:, part])

    inner = list(range(1, cells + 1))
    gradient_rows(h, (0, 1, 2, 3))
    image_shift(h, inner)
    for c in partner(1 - h):
        c.wait_recv()
    gradient_rows(1 - h, (0, 1, 2, 3))
    image_shift(1 - h, inner)
    image_rows(1, cells)

    @pl.when(k < count - 1)
    def _():
        for c, r in zip(down(), relay_above(h)):
            c.wait_recv()
            r.start()

    @pl.when(k > 0)
    def _():
        for c, r in zip(up(), relay_below(h)):
            c.wait_recv()
            r.start()

    contract(1, 2)

    @pl.when(k < count - 1)
    def _():
        for c in relay_above(1 - h):
            c.wait_recv()

    @pl.when(k > 0)
    def _():
        for c in relay_below(1 - h):
            c.wait_recv()

    for s in range(2):
        gradient_rows(s, (4,))
        image_shift(s, [0, cells + 1])
    image_rows(0, 1)
    image_rows(cells + 1, 1)
    contract(0, 1)
    contract(3, 1)

    deep, first = sums["kernel"], sums["first"]
    blocks = []
    for t, (pd_, pw, ph, sd, sh, sw) in sorted((t, key) for key, t in taps.items()):
        r = (pd_ * 4 + pw * 2 + ph) * 16
        c = (sd * 4 + sh * 2 + sw) * 32
        blocks.append(deep[r : r + 16, c : c + 32])
    total = jnp.zeros((16, 256), F32)
    bias = jnp.sum(sums["bias"], axis=1, keepdims=True)
    first_bias = jnp.zeros((16, 1), F32)
    for p in range(8):
        pd_, pw, ph = p // 4, (p // 2) % 2, p % 2
        move = pd_ * 64 + ph * 16 + pw * 4
        piece = first[p * 16 : p * 16 + 16]
        total = total + (pltpu.roll(piece, 256 - move, 1) if move else piece)
        first_bias = first_bias + bias[p * 16 : p * 16 + 16]
    deep_bias = jnp.sum(sums["deep"], axis=1, keepdims=True)
    lane = iota((16, 256), 1)
    total = jnp.where(lane == 12, first_bias, total)
    total = jnp.where(lane == 13, deep_bias[0:16], total)
    total = jnp.where(lane == 14, deep_bias[16:32], total)
    blocks.append(jnp.concatenate([total[:, 160:176], jnp.zeros((16, 16), F32)], axis=1))
    for q in range(7):
        src[q * 16 : q * 16 + 16, :] = jnp.concatenate(blocks[q * 4 : q * 4 + 4], axis=1)
    src[112:128, :] = jnp.concatenate([total[:, 0:48], total[:, 64:112], total[:, 128:160]], axis=1)
    if src.shape[0] > 128:
        src[128:, :] = jnp.zeros((src.shape[0] - 128, 128), F32)

    size = src.shape[0] // members

    def block(number):
        return pl.ds(pl.multiple_of(number * size, 8), size)

    def hop(src_ref, dst_ref, phase, j, number):
        return pltpu.make_async_remote_copy(
            src_ref=src_ref,
            dst_ref=dst_ref,
            send_sem=sems.at[2 * phase, j],
            recv_sem=sems.at[2 * phase + 1, j],
            device_id=device(number),
            device_id_type=MESH,
        )

    scatter = [hop(src.at[block(peers[j])], arrived.at[j], 0, j, peers[j]) for j in turns]
    for c in scatter:
        c.start()
    total = src[block(index), :]
    for j, c in reversed(list(zip(turns, scatter))):
        c.wait_recv()
        total = total + arrived[j]
    mine[...] = total
    whole[block(index), :] = total
    gather = [hop(mine, whole.at[block(index)], 1, j, peers[j]) for j in turns]
    for c in gather:
        c.start()

    for c in scatter + partner(h):
        c.wait_send()

    @pl.when(k > 0)
    def _():
        for c in down() + relay_below(h):
            c.wait_send()

    @pl.when(k < count - 1)
    def _():
        for c in up() + relay_above(h):
            c.wait_send()

    for j in turns:
        source = origin(j)
        hop(mine, whole.at[block(source)], 1, j, source).wait_recv()
    for c in gather:
        c.wait_send()


def fused(count, heights, hidden, images, pre_deep, pooled, weight):
    samples, chans, cells, rows, width = images.shape
    out_chans, coarse, coarse_rows, coarse_width = pre_deep.shape
    members = count * heights
    size = 8 * (-(-128 // (8 * members)))
    return pl.pallas_call(
        functools.partial(fused_kernel, count, heights),
        out_shape=jax.ShapeDtypeStruct((members * size, 128), F32),
        in_specs=[pl.BlockSpec(memory_space=pl.ANY)] * 5,
        out_specs=vmem(),
        scratch_shapes=[
            pltpu.VMEM(hidden.shape, BF),
            pltpu.VMEM(weight.shape, BF),
            pltpu.VMEM((2, samples, chans, cells + 2, rows, width), BF),
            pltpu.VMEM((2, out_chans, coarse + 1, coarse_rows, coarse_width), BF),
            pltpu.VMEM((2, 2) + pooled.shape, BF),
            pltpu.VMEM((128, 4096), BF),
            pltpu.VMEM((128, 4096), BF),
            pltpu.VMEM((256, 4096), BF),
            pltpu.VMEM((256, (cells + 2) * 256), BF),
            pltpu.VMEM((256, 4096), BF),
            pltpu.VMEM((members * size, 128), F32),
            pltpu.VMEM((members, size, 128), F32),
            pltpu.VMEM((size, 128), F32),
            pltpu.SemaphoreType.DMA((5,)),
            pltpu.SemaphoreType.DMA((11,)),
            pltpu.SemaphoreType.DMA((11,)),
            pltpu.SemaphoreType.DMA((4, members)),
        ],
        compiler_params=pltpu.CompilerParams(collective_id=0, has_side_effects=True),
    )(hidden, images, pre_deep, pooled, weight)


def unpack_kernel(whole, deep, first, deep_bias, first_bias):
    for t in range(27):
        r, c = (t // 4) * 16, (t % 4) * 32
        deep[t] = whole[r : r + 16, c : c + 32]
    flipped = jnp.transpose(whole[112:128, :])
    rest = jnp.transpose(whole[96:112, :])[96:112]
    for t in range(27):
        r = (t // 9) * 48 + ((t // 3) % 3) * 16 + (t % 3) * 4
        first[t] = flipped[r : r + 4] if r < 128 else rest[r - 128 : r - 124]
    first_bias[...] = flipped[12:13]
    deep_bias[...] = jnp.concatenate([flipped[13:14], flipped[14:15]], axis=1)


def unpack(whole):
    return pl.pallas_call(
        unpack_kernel,
        out_shape=(
            jax.ShapeDtypeStruct((27, 16, 32), F32),
            jax.ShapeDtypeStruct((27, 4, 16), F32),
            jax.ShapeDtypeStruct((1, 32), F32),
            jax.ShapeDtypeStruct((1, 16), F32),
        ),
        in_specs=[vmem()],
        out_specs=(vmem(),) * 4,
    )(whole)


def on_device(count, heights, images, pre_hidden, pre_deep, pooled_grad, deep_weight):
    weight = deep_weight.transpose(2, 3, 4, 1, 0).reshape(27, 16, 32)
    whole = fused(count, heights, pre_hidden, images, pre_deep[0], pooled_grad[0], weight)
    deep, first, deep_bias, first_bias = unpack(whole)
    return (
        first.reshape(3, 3, 3, 4, 16).transpose(4, 3, 0, 1, 2),
        first_bias.reshape(16),
        deep.reshape(3, 3, 3, 16, 32).transpose(4, 3, 0, 1, 2),
        deep_bias.reshape(32),
    )


def solution(mesh):
    return jax.shard_map(
        functools.partial(on_device, mesh.shape["depth"], mesh.shape["height"]),
        mesh=mesh,
        in_specs=(
            P("groups", None, "depth", "height", None),
            P("groups", None, "depth", "height", None),
            P(("groups", "height"), None, "depth", None, None),
            P(("groups", "height"), None, "depth", None),
            P(),
        ),
        out_specs=(
            P("groups", None, None, None, None),
            P("groups"),
            P("groups", None, None, None, None),
            P("groups"),
        ),
        check_vma=False,
    )
```

```python
import functools

import jax
import jax.numpy as jnp
from jax import lax
from jax.experimental import pallas as pl
from jax.experimental.pallas import tpu as pltpu
from jax.sharding import PartitionSpec as P

SLOPE = 0.3
MESH = pl.DeviceIdType.MESH
BF = jnp.bfloat16
F32 = jnp.float32
TAP = ((1, 1), (0, 0), (0, 1))


def vmem():
    return pl.BlockSpec(memory_space=pltpu.VMEM)


def iota(shape, dim):
    return lax.broadcasted_iota(jnp.int32, shape, dim)


def one_hot(row_target, shape):
    return jnp.where(row_target == iota(shape, 1), 1.0, 0.0).astype(BF)


def dot(a, b):
    return jnp.dot(a, b, preferred_element_type=F32)


def dot_nt(a, b):
    return lax.dot_general(a, b, (((1,), (1,)), ((), ())), preferred_element_type=F32)


def fused_kernel(
    count, heights, hid_in, img_in, pd_in, pool_in, weight_in, whole,
    hid, weight, img_all, pd_all, pool_all, ph_buf, f_buf, g_buf, y_buf, i_buf, src, arrived, mine,
    local, send, recv, sems,
):
    k = lax.axis_index("depth")
    h = lax.axis_index("height")
    members = count * heights
    index = k * heights + h
    cells = img_in.shape[2]
    quarter = pd_in.shape[1]

    def device(number):
        return {"depth": number // heights, "height": number % heights}

    def flipped(j):
        if members & (members - 1):
            return lax.rem(index + j, members)
        total, bit = 0, 1
        while bit < members:
            digit = (index // bit) % 2
            total = total + bit * (1 - digit if j & bit else digit)
            bit *= 2
        return total

    def origin(j):
        if members & (members - 1):
            return lax.rem(index + members - j, members)
        return flipped(j)

    turns = list(range(members - 1, 0, -1))
    peers = {j: flipped(j) for j in turns}
    barrier = pltpu.get_barrier_semaphore()
    for j in turns:
        pl.semaphore_signal(barrier, inc=1, device_id=device(peers[j]), device_id_type=MESH)

    loads = [
        pltpu.make_async_copy(hid_in, hid, local.at[0]),
        pltpu.make_async_copy(pd_in, pd_all.at[h, :, 0:quarter], local.at[1]),
        pltpu.make_async_copy(pool_in, pool_all.at[h, 0], local.at[2]),
        pltpu.make_async_copy(img_in, img_all.at[h, :, :, 1 : cells + 1], local.at[3]),
        pltpu.make_async_copy(weight_in, weight, local.at[4]),
    ]
    for c in loads:
        c.start()

    row = iota((128, 128), 0)
    order = one_hot((row & 15) * 8 + (row >> 4), (128, 128))
    z = iota((256, 256), 0)
    col = iota((256, 256), 1)
    split = jnp.where(z == 2 * (col & 127) + (col >> 7), 1.0, 0.0).astype(BF)

    def hidden_rows(s, d):
        x = hid[s, :, d].astype(F32).reshape(128, 256).astype(BF)
        a = dot(x, split).astype(BF)
        b = dot(order, a).astype(BF)
        for h2 in range(4):
            for pw in range(2):
                r = (d % 2) * 64 + pw * 32
                at = (d // 2) * 1024 + s * 512 + h2 * 128
                ph_buf[r : r + 32, at : at + 128] = b[
                    h2 * 32 : h2 * 32 + 32, pw * 128 : pw * 128 + 128
                ]

    loads[0].wait()
    for s in range(2):
        for d in range(8):
            hidden_rows(s, d)

    row = iota((160, 256), 0)
    high = 4 * h + (row >> 5)
    pick = one_hot(jnp.where(high < 8, (row & 31) * 8 + high, -1), (160, 256))
    r640 = iota((256, 640), 0)
    c640 = iota((256, 640), 1)
    spread_mat = jnp.where(
        r640 == ((4 * h + (c640 >> 7)) >> 1) * 64 + ((c640 & 127) >> 1), 1.0, 0.0
    ).astype(BF)
    z = iota((256, 512), 0)
    col = iota((256, 512), 1)
    shifts = jnp.where(z == 2 * (col & 127) + (col >> 7) - 1, 1.0, 0.0).astype(BF)
    high = 8 * h + (row >> 4) - 1
    target = ((row >> 2) & 3) * 64 + (high >> 3) * 32 + (row & 3) * 8 + (high & 7)
    lift = one_hot(jnp.where((high >= 0) & (high < 16), target, -1), (160, 256))
    lane = iota((32, 128), 1)
    for c in loads[1:]:
        c.wait()

    pl.semaphore_wait(barrier, members - 1)

    def copy(src_ref, dst_ref, slot, depth, height):
        return pltpu.make_async_remote_copy(
            src_ref=src_ref,
            dst_ref=dst_ref,
            send_sem=send.at[slot],
            recv_sem=recv.at[slot],
            device_id={"depth": depth, "height": height},
            device_id_type=MESH,
        )

    def same(part, slot):
        return copy(part, part, slot, k, 1 - h)

    def partner(slot):
        return [
            same(pd_all.at[slot, :, 0:quarter], 0),
            same(pool_all.at[slot, 0], 1),
            same(img_all.at[slot, :, :, 1 : cells + 1], 2),
        ]

    def down():
        return [
            copy(pd_all.at[h, :, 0:1], pd_all.at[h, :, quarter : quarter + 1], 3, k - 1, h),
            copy(pool_all.at[h, 0], pool_all.at[h, 1], 4, k - 1, h),
            copy(img_all.at[h, :, :, 1:2], img_all.at[h, :, :, cells + 1 : cells + 2], 5, k - 1, h),
        ]

    def up():
        return [copy(img_all.at[h, :, :, cells : cells + 1], img_all.at[h, :, :, 0:1], 6, k + 1, h)]

    def relay_above(slot):
        return [
            same(pd_all.at[slot, :, quarter : quarter + 1], 7),
            same(pool_all.at[slot, 1], 8),
            same(img_all.at[slot, :, :, cells + 1 : cells + 2], 9),
        ]

    def relay_below(slot):
        return [same(img_all.at[slot, :, :, 0:1], 10)]

    @pl.when(k > 0)
    def _():
        for c in down():
            c.start()

    @pl.when(k < count - 1)
    def _():
        for c in up():
            c.start()

    for c in partner(h):
        c.start()

    @pl.when(k == 0)
    def _():
        img_all[:, :, :, 0:1] = jnp.zeros_like(img_all[:, :, :, 0:1])

    @pl.when(k == count - 1)
    def _():
        img_all[:, :, :, cells + 1 : cells + 2] = jnp.zeros_like(img_all[:, :, :, 0:1])
        pd_all[:, :, quarter : quarter + 1] = jnp.zeros_like(pd_all[:, :, 0:1])
        pool_all[:, 1] = jnp.zeros_like(pool_all[:, 1])

    taps = {}
    for a in range(3):
        for b in range(3):
            for c in range(3):
                (sd, pd_), (sh, ph), (sw, pw) = TAP[a], TAP[b], TAP[c]
                taps[(pd_, pw, ph, sd, sh, sw)] = a * 9 + b * 3 + c
    bands = []
    zero = jnp.zeros((16, 32), F32)
    for p in range(8):
        phase = (p // 4, (p // 2) % 2, p % 2)
        pieces = []
        for s in range(8):
            t = taps.get(phase + (s // 4, (s // 2) % 2, s % 2))
            pieces.append(zero if t is None else weight[t].astype(F32))
        bands.append(jnp.concatenate(pieces, axis=1))
    matrix = jnp.concatenate(bands, axis=0).astype(BF)

    sums = {"deep": jnp.zeros((32, 128), F32)}

    def gradient_rows(s, depths):
        x = jnp.concatenate(
            [pd_all[s, :, d].astype(F32).reshape(256, 128).astype(BF) for d in depths], axis=1
        )
        y = dot(pick, x)
        coarse = pool_all[s, depths[0] // 4].astype(F32)
        halves = sorted({(d // 2) % 2 for d in depths})
        rows = jnp.concatenate([coarse[:, n, :] for n in halves], axis=0).astype(BF)
        spread = dot(rows, spread_mat) / 8.0
        for n, d in enumerate(depths):
            r = halves.index((d // 2) % 2) * 32
            for j in range(5):
                pre = y[j * 32 : j * 32 + 32, n * 128 : n * 128 + 128]
                slope = jnp.where(pre > 0, 1.0, SLOPE)
                g = (spread[r : r + 32, j * 128 : j * 128 + 128] * slope).astype(BF)
                wide = g.astype(F32)
                if d < 4 and j < 4:
                    sums["deep"] = sums["deep"] + wide
                moved = jnp.where(lane < 127, pltpu.roll(wide, 127, 1), 0.0).astype(BF)
                for sd in range(2):
                    for sh in range(2):
                        if 0 <= d - sd < 4 and 0 <= j - sh < 4:
                            at = pl.multiple_of((d - sd) * 1024 + s * 512 + (j - sh) * 128, 128)
                            r2 = (sd * 4 + sh * 2) * 32
                            g_buf[r2 : r2 + 32, pl.ds(at, 128)] = g
                            g_buf[r2 + 32 : r2 + 64, pl.ds(at, 128)] = moved

    def image_shift(half, depths):
        x = jnp.concatenate(
            [img_all[half, s, :, d].astype(F32).reshape(32, 256) for d in depths for s in range(2)], axis=0
        ).astype(BF)
        y = dot(x, shifts).astype(BF)
        for n, d in enumerate(depths):
            for s in range(2):
                r = (n * 2 + s) * 32
                at = (d * 2 + s) * 128
                for o in range(4):
                    low = pl.multiple_of(o * 64 + half * 32, 32)
                    y_buf[pl.ds(low, 32), at : at + 128] = y[r : r + 32, o * 128 : o * 128 + 128]

    def image_rows(first_depth, depths):
        at = first_depth * 256
        t = dot(lift, y_buf[:, at : at + 256 * depths]).astype(BF)
        for d in range(first_depth, first_depth + depths):
            for hh in range(10):
                for od in range(4):
                    for oh in range(4):
                        if (d - od) % 2 == 0 and (hh - oh) % 2 == 0:
                            d2, h2 = (d - od) // 2, (hh - oh) // 2
                            if 0 <= d2 < 4 and 0 <= h2 < 4:
                                r = (od * 4 + oh) * 16
                                for s in range(2):
                                    to = d2 * 1024 + s * 512 + h2 * 128
                                    c = ((d - first_depth) * 2 + s) * 128
                                    i_buf[r : r + 16, to : to + 128] = t[
                                        hh * 16 : hh * 16 + 16, c : c + 128
                                    ]

    sums["kernel"] = jnp.zeros((128, 256), F32)
    sums["first"] = jnp.zeros((128, 256), F32)
    sums["bias"] = jnp.zeros((128, 128), F32)

    def contract(d2, blocks):
        for at in range(d2 * 1024, (d2 + blocks) * 1024, 512):
            part = slice(at, at + 512)
            pre = ph_buf[:, part].astype(F32)
            grad = dot(matrix, g_buf[:, part]).astype(BF).astype(F32)
            grad = (grad * jnp.where(pre > 0, 1.0, SLOPE)).astype(BF)
            ph_buf[:, part] = jnp.where(pre > 0, pre, SLOPE * pre).astype(BF)
            f_buf[:, part] = grad
            wide = grad.astype(F32)
            for o in range(0, 512, 128):
                sums["bias"] = sums["bias"] + wide[:, o : o + 128]
        part = slice(d2 * 1024, (d2 + blocks) * 1024)
        sums["kernel"] = sums["kernel"] + dot_nt(ph_buf[:, part], g_buf[:, part])
        sums["first"] = sums["first"] + dot_nt(f_buf[:, part], i_buf[:, part])

    inner = list(range(1, cells + 1))
    gradient_rows(h, (0, 1, 2, 3))
    image_shift(h, inner)
    for c in partner(1 - h):
        c.wait_recv()
    gradient_rows(1 - h, (0, 1, 2, 3))
    image_shift(1 - h, inner)
    image_rows(1, cells)

    @pl.when(k < count - 1)
    def _():
        for c, r in zip(down(), relay_above(h)):
            c.wait_recv()
            r.start()

    @pl.when(k > 0)
    def _():
        for c, r in zip(up(), relay_below(h)):
            c.wait_recv()
            r.start()

    contract(1, 2)

    @pl.when(k < count - 1)
    def _():
        for c in relay_above(1 - h):
            c.wait_recv()

    @pl.when(k > 0)
    def _():
        for c in relay_below(1 - h):
            c.wait_recv()

    for s in range(2):
        gradient_rows(s, (4,))
        image_shift(s, [0, cells + 1])
    image_rows(0, 1)
    image_rows(cells + 1, 1)
    contract(0, 1)
    contract(3, 1)

    deep, first = sums["kernel"], sums["first"]
    blocks = []
    for t, (pd_, pw, ph, sd, sh, sw) in sorted((t, key) for key, t in taps.items()):
        r = (pd_ * 4 + pw * 2 + ph) * 16
        c = (sd * 4 + sh * 2 + sw) * 32
        blocks.append(deep[r : r + 16, c : c + 32])
    total = jnp.zeros((16, 256), F32)
    bias = jnp.sum(sums["bias"], axis=1, keepdims=True)
    first_bias = jnp.zeros((16, 1), F32)
    for p in range(8):
        pd_, pw, ph = p // 4, (p // 2) % 2, p % 2
        move = pd_ * 64 + ph * 16 + pw * 4
        piece = first[p * 16 : p * 16 + 16]
        total = total + (pltpu.roll(piece, 256 - move, 1) if move else piece)
        first_bias = first_bias + bias[p * 16 : p * 16 + 16]
    deep_bias = jnp.sum(sums["deep"], axis=1, keepdims=True)
    lane = iota((16, 256), 1)
    total = jnp.where(lane == 12, first_bias, total)
    total = jnp.where(lane == 13, deep_bias[0:16], total)
    total = jnp.where(lane == 14, deep_bias[16:32], total)
    blocks.append(jnp.concatenate([total[:, 160:176], jnp.zeros((16, 16), F32)], axis=1))
    for q in range(7):
        src[q * 16 : q * 16 + 16, :] = jnp.concatenate(blocks[q * 4 : q * 4 + 4], axis=1)
    src[112:128, :] = jnp.concatenate([total[:, 0:48], total[:, 64:112], total[:, 128:160]], axis=1)
    if src.shape[0] > 128:
        src[128:, :] = jnp.zeros((src.shape[0] - 128, 128), F32)

    size = src.shape[0] // members

    def block(number):
        return pl.ds(pl.multiple_of(number * size, 8), size)

    def hop(src_ref, dst_ref, phase, j, number):
        return pltpu.make_async_remote_copy(
            src_ref=src_ref,
            dst_ref=dst_ref,
            send_sem=sems.at[2 * phase, j],
            recv_sem=sems.at[2 * phase + 1, j],
            device_id=device(number),
            device_id_type=MESH,
        )

    scatter = [hop(src.at[block(peers[j])], arrived.at[j], 0, j, peers[j]) for j in turns]
    for c in scatter:
        c.start()
    total = src[block(index), :]
    for j, c in reversed(list(zip(turns, scatter))):
        c.wait_recv()
        total = total + arrived[j]
    mine[...] = total.astype(BF)
    whole[index] = total.astype(BF)
    gather = [hop(mine, whole.at[index], 1, j, peers[j]) for j in turns]
    for c in gather:
        c.start()

    for c in scatter + partner(h):
        c.wait_send()

    @pl.when(k > 0)
    def _():
        for c in down() + relay_below(h):
            c.wait_send()

    @pl.when(k < count - 1)
    def _():
        for c in up() + relay_above(h):
            c.wait_send()

    for j in turns:
        source = origin(j)
        hop(mine, whole.at[source], 1, j, source).wait_recv()
    for c in gather:
        c.wait_send()


def fused(count, heights, hidden, images, pre_deep, pooled, weight):
    samples, chans, cells, rows, width = images.shape
    out_chans, coarse, coarse_rows, coarse_width = pre_deep.shape
    members = count * heights
    size = 8 * (-(-128 // (8 * members)))
    return pl.pallas_call(
        functools.partial(fused_kernel, count, heights),
        out_shape=jax.ShapeDtypeStruct((members, size, 128), BF),
        in_specs=[pl.BlockSpec(memory_space=pl.ANY)] * 5,
        out_specs=vmem(),
        scratch_shapes=[
            pltpu.VMEM(hidden.shape, BF),
            pltpu.VMEM(weight.shape, BF),
            pltpu.VMEM((2, samples, chans, cells + 2, rows, width), BF),
            pltpu.VMEM((2, out_chans, coarse + 1, coarse_rows, coarse_width), BF),
            pltpu.VMEM((2, 2) + pooled.shape, BF),
            pltpu.VMEM((128, 4096), BF),
            pltpu.VMEM((128, 4096), BF),
            pltpu.VMEM((256, 4096), BF),
            pltpu.VMEM((256, (cells + 2) * 256), BF),
            pltpu.VMEM((256, 4096), BF),
            pltpu.VMEM((members * size, 128), F32),
            pltpu.VMEM((members, size, 128), F32),
            pltpu.VMEM((size, 128), BF),
            pltpu.SemaphoreType.DMA((5,)),
            pltpu.SemaphoreType.DMA((11,)),
            pltpu.SemaphoreType.DMA((11,)),
            pltpu.SemaphoreType.DMA((4, members)),
        ],
        compiler_params=pltpu.CompilerParams(collective_id=0, has_side_effects=True),
    )(hidden, images, pre_deep, pooled, weight)


def unpack_kernel(gathered, deep, first, deep_bias, first_bias):
    whole = gathered[...].astype(F32).reshape(-1, 128)
    for t in range(27):
        r, c = (t // 4) * 16, (t % 4) * 32
        deep[t] = whole[r : r + 16, c : c + 32]
    flipped = jnp.transpose(whole[112:128, :])
    rest = jnp.transpose(whole[96:112, :])[96:112]
    for t in range(27):
        r = (t // 9) * 48 + ((t // 3) % 3) * 16 + (t % 3) * 4
        first[t] = flipped[r : r + 4] if r < 128 else rest[r - 128 : r - 124]
    first_bias[...] = flipped[12:13]
    deep_bias[...] = jnp.concatenate([flipped[13:14], flipped[14:15]], axis=1)


def unpack(whole):
    return pl.pallas_call(
        unpack_kernel,
        out_shape=(
            jax.ShapeDtypeStruct((27, 16, 32), F32),
            jax.ShapeDtypeStruct((27, 4, 16), F32),
            jax.ShapeDtypeStruct((1, 32), F32),
            jax.ShapeDtypeStruct((1, 16), F32),
        ),
        in_specs=[vmem()],
        out_specs=(vmem(),) * 4,
    )(whole)


def on_device(count, heights, images, pre_hidden, pre_deep, pooled_grad, deep_weight):
    weight = deep_weight.transpose(2, 3, 4, 1, 0).reshape(27, 16, 32)
    whole = fused(count, heights, pre_hidden, images, pre_deep[0], pooled_grad[0], weight)
    deep, first, deep_bias, first_bias = unpack(whole)
    return (
        first.reshape(3, 3, 3, 4, 16).transpose(4, 3, 0, 1, 2),
        first_bias.reshape(16),
        deep.reshape(3, 3, 3, 16, 32).transpose(4, 3, 0, 1, 2),
        deep_bias.reshape(32),
    )


def solution(mesh):
    return jax.shard_map(
        functools.partial(on_device, mesh.shape["depth"], mesh.shape["height"]),
        mesh=mesh,
        in_specs=(
            P("groups", None, "depth", "height", None),
            P("groups", None, "depth", "height", None),
            P(("groups", "height"), None, "depth", None, None),
            P(("groups", "height"), None, "depth", None),
            P(),
        ),
        out_specs=(
            P("groups", None, None, None, None),
            P("groups"),
            P("groups", None, None, None, None),
            P("groups"),
        ),
        check_vma=False,
    )
```
